32 devices in a mesh: dp: 4 (over y, x), ctx: 8 (over z, core).
Axes of the slice: x: 2, y: 2, z: 4, core: 2. Of those that a mesh axis runs over, the one named last changes fastest.
Arguments:
- q_proj: bfloat16 [4, 1024, 2048], P('dp', 'ctx'), may hold values from -80 to 80
- k_proj: bfloat16 [4, 1024, 1024], P('dp', 'ctx'), may hold values from -80 to 80
- v_proj: bfloat16 [4, 1024, 1024], P('dp', 'ctx'), may hold values from -6 to 6
- d_out: bfloat16 [4, 1024, 2048], P('dp', 'ctx'), may hold values from -7 to 7
- q_gain: float32 [128], replicated, may hold values from 0.5 to 9
- k_gain: float32 [128], replicated, may hold values from 0.5 to 9
Outputs:
- attn_out: bfloat16 [4, 1024, 2048], P('dp', 'ctx')
- d_q_proj: bfloat16 [4, 1024, 2048], P('dp', 'ctx')
- d_k_proj: bfloat16 [4, 1024, 1024], P('dp', 'ctx')
- d_v_proj: bfloat16 [4, 1024, 1024], P('dp', 'ctx')
- gain_grads: float32 [256], P('dp')
The draws below stay inside these ranges and needn't reach their ends.
All inputs are finite; a program needn't handle non-finite values.
Results may differ from the reference program's by a relative error of at most 0.017.
The reference program's roundings to bfloat16 on the way count: a program that leaves them out, or rounds other values in their place, can miss the bound.
Values may be sent and summed in bfloat16 or wider, within the bound.
No kernel may reach another device: no remote copies, remote signals or barrier semaphores. Data moves between devices by JAX's collectives and lax.ppermute only.
A program may use at most 64 MiB of HBM per device.

```python
import math
import jax
import jax.numpy as jnp
from jax import lax

HQ = 16
HK = 8
HD = 128
TOK_DEV = 128
WINDOW = 256
LENGTH = 1024
DOCS = 4
N_CTX = 8


def query_key_pair(key):
    keys = jax.random.split(jax.random.fold_in(key, 17), 6)
    q_shape = (DOCS, LENGTH, HQ, HD)
    k_shape = (DOCS, LENGTH, HK, HD)
    q_base = jnp.clip(jax.random.normal(keys[0], q_shape, jnp.float32), -4.0, 4.0)
    k_base = jnp.clip(jax.random.normal(keys[1], k_shape, jnp.float32), -4.0, 4.0)
    q_rows = jnp.exp(jax.random.uniform(keys[2], (DOCS, LENGTH, HQ, 1), jnp.float32, 0.0, math.log(10.0)))
    k_rows = jnp.exp(jax.random.uniform(keys[3], (DOCS, LENGTH, HK, 1), jnp.float32, 0.0, math.log(10.0)))
    q_cols = jnp.exp(jax.random.uniform(keys[4], (HD,), jnp.float32, 0.0, math.log(10.0)))
    k_cols = jnp.exp(jax.random.uniform(keys[5], (HD,), jnp.float32, 0.0, math.log(10.0)))
    queries = 0.15 * q_base * q_rows * q_cols
    keys_out = 0.15 * k_base * k_rows * k_cols
    return (queries.reshape(DOCS, LENGTH, HQ * HD), keys_out.reshape(DOCS, LENGTH, HK * HD))


def draw_q_proj(key, part):
    return query_key_pair(key)[0].astype(jnp.bfloat16)


def draw_k_proj(key, part):
    return query_key_pair(key)[1].astype(jnp.bfloat16)


def draw_d_out(key, part):
    keys = jax.random.split(jax.random.fold_in(key, 29), 1)
    shape = (DOCS, LENGTH, HQ * HD)
    ramp = (jnp.arange(LENGTH, dtype=jnp.float32) / LENGTH)[None, :, None]
    base = jnp.clip(jax.random.normal(keys[0], shape, jnp.float32), -4.0, 4.0)
    result = base * (0.5 + ramp)
    return result.astype(jnp.bfloat16)


def gain_draw(key, salt):
    inner = jax.random.fold_in(key, salt)
    return jnp.exp(jax.random.uniform(inner, (HD,), jnp.float32, math.log(0.5), math.log(2.0)))


def draw_q_gain(key, part):
    return gain_draw(key, 41)


def draw_k_gain(key, part):
    return gain_draw(key, 43)


def block_levels(rng, extent, shards, smallest, high):
    def one(dim, shards_of):
        heights = jax.random.uniform(jax.random.fold_in(jax.random.fold_in(rng, 6), dim), (shards_of,), jnp.float32, smallest / len(shards), high / len(shards))
        return jnp.repeat(jnp.exp(heights), extent[dim] // shards_of).reshape((-1,) + (1,) * (len(extent) - dim - 1))

    factor_of = one(*shards[0])
    for cut in shards[1:]:
        factor_of = factor_of * one(*cut)
    return factor_of


def gaussian(own_key, shape, spread, bound, pieces=(), kind=jnp.bfloat16):
    level = block_levels(own_key, shape, pieces, -0.22, 0.18) if pieces else 1.0
    entries = jax.random.normal(own_key, shape, jnp.float32) * spread * level
    return jnp.minimum(jnp.maximum(entries, -bound), bound).astype(kind)


def setup_inputs(seed: int = 0) -> dict:
    seeds = jax.random.split(jax.random.key(seed), 7)
    return {
        "q_proj": draw_q_proj(jax.random.fold_in(seeds[6], 71), 0),
        "k_proj": draw_k_proj(jax.random.fold_in(seeds[6], 71), 0),
        "v_proj": gaussian(seeds[2], (DOCS, LENGTH, HK * HD), 1.0, 6.0, ((0, 4), (1, 8))),
        "d_out": draw_d_out(jax.random.fold_in(seeds[6], 71), 0),
        "q_gain": draw_q_gain(jax.random.fold_in(seeds[6], 71), 0),
        "k_gain": draw_k_gain(jax.random.fold_in(seeds[6], 71), 0),
    }


EPSILON = 1e-06
ROPE_BASE = 10000.0
SCORE_SCALE = 168.0 ** (-0.5)

def norm_rope(values, gain, positions):
    mean_sq = lax.optimization_barrier(jnp.mean(values * values, axis=-1, keepdims=True))
    normed = values * lax.rsqrt(mean_sq + EPSILON) * gain
    half_size = values.shape[-1] // 2
    freqs = jnp.power(ROPE_BASE, -2.0 * jnp.arange(half_size, dtype=jnp.float32) / values.shape[-1])
    angles = positions.astype(jnp.float32)[:, None, None] * freqs
    cosine = jnp.cos(angles)
    sine = jnp.sin(angles)
    first = normed[..., :half_size]
    second = normed[..., half_size:]
    return jnp.concatenate([first * cosine - second * sine, second * cosine + first * sine], axis=-1)

def attend(queries, keys, values, grad_out, visible):
    scores = jnp.einsum('tkgd,ekd->kgte', queries, keys) * SCORE_SCALE
    masked = jnp.where(visible, scores, -1e+30)
    highest = lax.optimization_barrier(jnp.max(masked, axis=-1, keepdims=True))
    exponent = jnp.exp(masked - highest)
    probabilities = exponent / lax.optimization_barrier(jnp.sum(exponent, axis=-1, keepdims=True))
    probs_b = lax.optimization_barrier(probabilities.astype(jnp.bfloat16)).astype(jnp.float32)
    result = jnp.einsum('kgte,ekd->tkgd', probs_b, values)
    d_prob = jnp.einsum('tkgd,ekd->kgte', grad_out, values)
    delta = lax.optimization_barrier(jnp.sum(probabilities * d_prob, axis=-1, keepdims=True))
    d_score = probabilities * (d_prob - delta) * SCORE_SCALE
    d_score = lax.optimization_barrier(d_score.astype(jnp.bfloat16)).astype(jnp.float32)
    d_query = jnp.einsum('kgte,ekd->tkgd', d_score, keys)
    d_key = jnp.einsum('kgte,tkgd->ekd', d_score, queries)
    d_value = jnp.einsum('kgte,tkgd->ekd', probs_b, grad_out)
    return (result, d_query, d_key, d_value)

def reference(q_proj, k_proj, v_proj, d_out, q_gain, k_gain):
    group_size = HQ // HK
    key_span = WINDOW + TOK_DEV
    width = HK * HD

    def one_document(tensors):
        q_doc, k_doc, v_doc, dout_doc = tensors
        positions = jnp.arange(LENGTH, dtype=jnp.int32)
        q_float = q_doc.astype(jnp.float32).reshape(LENGTH, HQ, HD)
        k_float = k_doc.astype(jnp.float32).reshape(LENGTH, HK, HD)
        q_rot = lax.optimization_barrier(norm_rope(q_float, q_gain, positions).astype(jnp.bfloat16)).reshape(LENGTH, HQ * HD)
        k_rot = lax.optimization_barrier(norm_rope(k_float, k_gain, positions).astype(jnp.bfloat16)).reshape(LENGTH, width)
        joined = jnp.concatenate([k_rot, v_doc], axis=1)
        padded = jnp.concatenate([jnp.zeros((WINDOW, 2 * width), jnp.bfloat16), joined], axis=0)
        buffer = jnp.zeros((WINDOW + LENGTH, 2 * width), jnp.float32)
        row_ids = jnp.arange(TOK_DEV, dtype=jnp.int32)[:, None]
        key_ids = jnp.arange(key_span, dtype=jnp.int32)[None, :]

        def per_shard(accum, shard):
            first_row = (shard * TOK_DEV).astype(jnp.int32)
            q_rows = lax.dynamic_slice_in_dim(q_rot, first_row, TOK_DEV, 0)
            dout_rows = lax.dynamic_slice_in_dim(dout_doc, first_row, TOK_DEV, 0)
            extended = lax.dynamic_slice_in_dim(padded, first_row, key_span, 0)
            visible = (key_ids > row_ids) & (key_ids <= row_ids + WINDOW) & (key_ids + first_row - WINDOW >= 0)
            queries = q_rows.astype(jnp.float32).reshape(TOK_DEV, HK, group_size, HD)
            keys = extended[:, :width].astype(jnp.float32).reshape(key_span, HK, HD)
            values = extended[:, width:].astype(jnp.float32).reshape(key_span, HK, HD)
            grad_out = dout_rows.astype(jnp.float32).reshape(TOK_DEV, HK, group_size, HD)
            result, d_query, d_key, d_value = attend(queries, keys, values, grad_out, visible)
            grads_ext = jnp.concatenate([d_key.reshape(key_span, width), d_value.reshape(key_span, width)], axis=1)
            tail_part = lax.optimization_barrier(grads_ext[:WINDOW].astype(jnp.bfloat16)).astype(jnp.float32)
            update = jnp.concatenate([tail_part, grads_ext[WINDOW:]], axis=0)
            current = lax.dynamic_slice_in_dim(accum, first_row, key_span, 0)
            accum = lax.dynamic_update_slice_in_dim(accum, current + update, first_row, 0)
            return (accum, (result.astype(jnp.bfloat16).reshape(TOK_DEV, HQ * HD), d_query.reshape(TOK_DEV, HQ, HD)))
        buffer, (outputs, d_queries) = lax.scan(per_shard, buffer, jnp.arange(N_CTX, dtype=jnp.int32))
        summed = buffer[WINDOW:]
        d_k_rot = summed[:, :width].reshape(LENGTH, HK, HD)
        d_value_doc = summed[:, width:].astype(jnp.bfloat16)
        d_q_rot = d_queries.reshape(LENGTH, HQ, HD)

        def q_side(values, gain):
            return norm_rope(values, gain, positions)
        _, q_back = jax.vjp(q_side, q_float, q_gain)
        d_q_in, d_q_gain = q_back(d_q_rot)
        _, k_back = jax.vjp(q_side, k_float, k_gain)
        d_k_in, d_k_gain = k_back(d_k_rot)
        return (outputs.reshape(LENGTH, HQ * HD), d_q_in.astype(jnp.bfloat16).reshape(LENGTH, HQ * HD), d_k_in.astype(jnp.bfloat16).reshape(LENGTH, width), d_value_doc, d_q_gain, d_k_gain)
    attn_out, d_q_proj, d_k_proj, d_v_proj, q_gain_grads, k_gain_grads = lax.map(one_document, (q_proj, k_proj, v_proj, d_out))
    gain_grads = jnp.concatenate([lax.optimization_barrier(jnp.sum(q_gain_grads, axis=0)), lax.optimization_barrier(jnp.sum(k_gain_grads, axis=0))])
    return (attn_out, d_q_proj, d_k_proj, d_v_proj, gain_grads)
```

```python
import math

import jax
import jax.numpy as jnp
from jax import lax
from jax.experimental import pallas as pl
from jax.experimental.pallas import tpu as pltpu
from jax.sharding import PartitionSpec as P

WINDOW = 256
EPSILON = 1e-06
ROPE_BASE = 10000.0
SCORE_SCALE = 168.0 ** (-0.5)
LOG2_SCALE = SCORE_SCALE * math.log2(math.e)
HIDDEN = -1e30
GROUP = 2
F32 = jnp.float32
BF16 = jnp.bfloat16


def hop(value, steps):
    count = lax.axis_size("ctx")
    initial, last = (max(0, -steps), min(count, count - steps))
    return lax.ppermute(value, "ctx", [(i, i + steps) for i in range(initial, last)])


def unit(x):
    inverse = lax.rsqrt(jnp.mean(x * x, axis=-1, keepdims=True) + EPSILON)
    return x * inverse, inverse


def rotate(y, cosine, sine):
    return y * cosine + pltpu.roll(y, y.shape[-1] // 2, 1) * sine


def unrotate(d, cosine, sine):
    return d * cosine + pltpu.roll(d * sine, d.shape[-1] // 2, 1)


def unit_back(d_y, normed, inverse, gain):
    d_normed = d_y * gain
    return inverse * (d_normed - normed * jnp.mean(d_normed * normed, axis=-1, keepdims=True))


def fold(x):
    return jnp.sum(x.reshape(-1, 8, x.shape[-1]), axis=0)


def dot(a, b, dims):
    return lax.dot_general(a, b, (dims, ((), ())), preferred_element_type=F32)


def attention_kernel(
    q_ref, do_ref, k0_ref, k1_ref, k2_ref, v0_ref, v1_ref, v2_ref, cos_ref, sin_ref, bias_ref, gain_ref,
    out_ref, dq_ref, own_ref, t1_ref, t2_ref, dg_ref,
):
    rows = q_ref.shape[0]
    head = gain_ref.shape[1]
    q_gain = gain_ref[0:1, :]
    k_gain = gain_ref[1:2, :]
    cosine = cos_ref[...]
    sine = sin_ref[...]
    span = cosine.shape[0]
    q_cos = jnp.concatenate([cosine[span - rows :]] * GROUP, axis=0)
    q_sin = jnp.concatenate([sine[span - rows :]] * GROUP, axis=0)

    def stacked(ref):
        return jnp.concatenate([ref[:, j * head : (j + 1) * head] for j in range(GROUP)], axis=0)

    q_unit, q_inv = unit(stacked(q_ref).astype(F32))
    queries = rotate(q_unit * q_gain, q_cos, q_sin).astype(BF16)
    grad_out = stacked(do_ref)
    k_raw = jnp.concatenate([k2_ref[...], k1_ref[...], k0_ref[...]], axis=0).astype(F32)
    k_unit, _ = unit(k_raw)
    keys = rotate(k_unit * k_gain, cosine, sine).astype(BF16)
    values = jnp.concatenate([v2_ref[...], v1_ref[...], v0_ref[...]], axis=0)

    bias = bias_ref[...]
    scores = dot(keys, queries, ((1,), (1,))) + jnp.concatenate([bias] * GROUP, axis=1)
    d_prob = dot(values, grad_out, ((1,), (1,)))
    top = jnp.max(scores, axis=0, keepdims=True)
    exps = jnp.exp2((scores - top) * LOG2_SCALE)
    probs = exps * (1.0 / jnp.sum(exps, axis=0, keepdims=True))
    probs_b = probs.astype(BF16)
    delta = jnp.sum(probs * d_prob, axis=0, keepdims=True)
    d_score = (probs * (d_prob - delta) * SCORE_SCALE).astype(BF16)

    result = dot(probs_b, values, ((0,), (0,)))
    d_query = dot(d_score, keys, ((0,), (0,)))
    d_key = dot(d_score, queries, ((1,), (0,)))
    d_value = dot(probs_b, grad_out, ((1,), (0,)))

    far = span - rows
    t1 = d_key[far - rows : far].astype(BF16)
    t2 = d_key[: far - rows].astype(BF16)
    own_ref[0] = d_key[far:]
    own_ref[1] = d_value[far:]
    t1_ref[0] = t1
    t1_ref[1] = d_value[far - rows : far].astype(BF16)
    t2_ref[0] = t2
    t2_ref[1] = d_value[: far - rows].astype(BF16)

    d_q_y = unrotate(d_query, q_cos, q_sin)
    d_q_in = unit_back(d_q_y, q_unit, q_inv, q_gain).astype(BF16)
    for j in range(GROUP):
        out_ref[:, j * head : (j + 1) * head] = result[j * rows : (j + 1) * rows].astype(BF16)
        dq_ref[:, j * head : (j + 1) * head] = d_q_in[j * rows : (j + 1) * rows]
    d_k_terms = jnp.concatenate([t2.astype(F32), t1.astype(F32), d_key[far:]], axis=0)
    d_k_y = unrotate(d_k_terms, cosine, sine)

    @pl.when(pl.program_id(0) == 0)
    def _():
        dg_ref[...] = jnp.zeros_like(dg_ref)

    dg_ref[0:8, :] += fold(d_q_y * q_unit)
    dg_ref[8:16, :] += fold(d_k_y * k_unit)


def attention(q, d_out, ks, vs, cosine, sine, bias, gains):
    rows = q.shape[0]
    head = gains.shape[1]
    heads = ks[0].shape[1] // head
    span = cosine.shape[0]
    wide = pl.BlockSpec((rows, GROUP * head), lambda h: (0, h))
    narrow = pl.BlockSpec((rows, head), lambda h: (0, h))
    pair = pl.BlockSpec((2, rows, head), lambda h: (0, 0, h))

    def fixed(shape):
        return pl.BlockSpec(shape, lambda h: (0, 0))

    flops = 6 * 2 * heads * GROUP * rows * span * head
    return pl.pallas_call(
        attention_kernel,
        name="attention",
        grid=(heads,),
        in_specs=[wide, wide] + [narrow] * 6
        + [fixed((span, head)), fixed((span, head)), fixed((span, rows)), fixed(gains.shape)],
        out_specs=[wide, wide, pair, pair, pair, fixed((16, head))],
        out_shape=[
            jax.ShapeDtypeStruct(q.shape, BF16),
            jax.ShapeDtypeStruct(q.shape, BF16),
            jax.ShapeDtypeStruct((2, rows, heads * head), F32),
            jax.ShapeDtypeStruct((2, rows, heads * head), BF16),
            jax.ShapeDtypeStruct((2, rows, heads * head), BF16),
            jax.ShapeDtypeStruct((16, head), F32),
        ],
        cost_estimate=pl.CostEstimate(flops=flops, bytes_accessed=6_000_000, transcendentals=0),
        compiler_params=pltpu.CompilerParams(vmem_limit_bytes=32 * 1024 * 1024),
    )(q, d_out, *ks, *vs, cosine, sine, bias, gains)


def finish_kernel(own_ref, a1_ref, a2_ref, k_ref, cos_ref, sin_ref, gain_ref, dk_ref, dv_ref):
    head = gain_ref.shape[1]
    rows = k_ref.shape[0]
    span = cos_ref.shape[0]
    cosine = cos_ref[span - rows :, :]
    sine = sin_ref[span - rows :, :]
    dv_ref[...] = (own_ref[1] + a1_ref[1].astype(F32) + a2_ref[1].astype(F32)).astype(BF16)
    for j in range(k_ref.shape[1] // head):
        cols = slice(j * head, (j + 1) * head)
        d_k = own_ref[0, :, cols] + a1_ref[0, :, cols].astype(F32) + a2_ref[0, :, cols].astype(F32)
        k_unit, k_inv = unit(k_ref[:, cols].astype(F32))
        d_y = unrotate(d_k, cosine, sine)
        dk_ref[:, cols] = unit_back(d_y, k_unit, k_inv, gain_ref[1:2, :]).astype(BF16)


def finish(own, a1, a2, k, cosine, sine, gains):
    rows, width = k.shape
    head = gains.shape[1]
    step = 2 * head
    narrow = pl.BlockSpec((rows, step), lambda h: (0, h))
    pair = pl.BlockSpec((2, rows, step), lambda h: (0, 0, h))

    def fixed(shape):
        return pl.BlockSpec(shape, lambda h: (0, 0))

    return pl.pallas_call(
        finish_kernel,
        name="finish",
        grid=(width // step,),
        in_specs=[pair] * 3 + [narrow, fixed(cosine.shape), fixed(sine.shape), fixed(gains.shape)],
        out_specs=[narrow, narrow],
        out_shape=[jax.ShapeDtypeStruct(k.shape, BF16)] * 2,
        cost_estimate=pl.CostEstimate(flops=20 * rows * width, bytes_accessed=3_000_000, transcendentals=0),
        compiler_params=pltpu.CompilerParams(vmem_limit_bytes=32 * 1024 * 1024),
    )(own, a1, a2, k, cosine, sine, gains)


def all_sum(value, axis):
    count = lax.axis_size(axis)
    step = 1
    while step < count:
        value = value + lax.ppermute(value, axis, [(i, i ^ step) for i in range(count)])
        step *= 2
    return value


def on_device(q_proj, k_proj, v_proj, d_out, q_gain, k_gain):
    rows = q_proj.shape[1]
    head = q_gain.shape[0]
    blocks = WINDOW // rows
    span = WINDOW + rows
    first_row = lax.axis_index("ctx") * rows
    k1, v1 = hop(k_proj, 1), hop(v_proj, 1)
    k2, v2 = hop(k_proj, 2), hop(v_proj, 2)

    half = head // 2
    freqs = jnp.power(ROPE_BASE, -2.0 * jnp.arange(half, dtype=F32) / head)
    positions = first_row - WINDOW + jnp.arange(span, dtype=jnp.int32)
    angles = positions.astype(F32)[:, None] * freqs
    cosine = jnp.cos(angles)
    sine = jnp.sin(angles)
    cosine = jnp.concatenate([cosine, cosine], axis=1)
    sine = jnp.concatenate([-sine, sine], axis=1)
    row_ids = jnp.arange(rows, dtype=jnp.int32)[None, :]
    key_ids = jnp.arange(span, dtype=jnp.int32)[:, None]
    visible = (key_ids > row_ids) & (key_ids <= row_ids + WINDOW) & (key_ids + first_row - WINDOW >= 0)
    bias = jnp.where(visible, 0.0, HIDDEN).astype(F32)
    gains = jnp.stack([q_gain, k_gain])

    result, d_q, own, t1, t2, terms = attention(
        q_proj[0], d_out[0], (k_proj[0], k1[0], k2[0]), (v_proj[0], v1[0], v2[0]), cosine, sine, bias, gains
    )
    a1 = hop(t1, -1)
    a2 = hop(t2, -2)
    d_k, d_v = finish(own, a1, a2, k_proj[0], cosine, sine, gains)
    gain_terms = jnp.sum(terms.reshape(2, 8, head), axis=1).reshape(2 * head)
    gain_terms = all_sum(all_sum(gain_terms, "dp"), "ctx")
    share = gain_terms.shape[0] // lax.axis_size("dp")
    gain_share = lax.dynamic_slice_in_dim(gain_terms, lax.axis_index("dp") * share, share, 0)
    return (result[None], d_q[None], d_k[None], d_v[None], gain_share)


def solution(mesh):
    tokens = P("dp", "ctx", None)
    return jax.shard_map(
        on_device,
        mesh=mesh,
        in_specs=(tokens,) * 4 + (P(), P()),
        out_specs=(tokens,) * 4 + (P("dp"),),
        check_vma=False,
    )
```

```python
import math

import jax
import jax.numpy as jnp
from jax import lax
from jax.experimental import pallas as pl
from jax.experimental.pallas import tpu as pltpu
from jax.sharding import PartitionSpec as P

WINDOW = 256
EPSILON = 1e-06
ROPE_BASE = 10000.0
SCORE_SCALE = 168.0 ** (-0.5)
LOG2_SCALE = SCORE_SCALE * math.log2(math.e)
HIDDEN = -1e30
GROUP = 2
F32 = jnp.float32
BF16 = jnp.bfloat16
UNROLL = 8
TABLES_COST = 10_000_000_000
IN_VMEM = pl.BlockSpec(memory_space=pltpu.VMEM)
VMEM_LIMIT = 24 * 1024 * 1024


def hop(value, steps):
    count = lax.axis_size("ctx")
    initial, last = (max(0, -steps), min(count, count - steps))
    return lax.ppermute(value, "ctx", [(i, i + steps) for i in range(initial, last)])


def ring_hop(value, steps):
    count = lax.axis_size("ctx")
    return lax.ppermute(value, "ctx", [(i, (i + steps) % count) for i in range(count)])


def swap_pairs(value):
    return lax.ppermute(value, "ctx", [(i, i ^ 1) for i in range(lax.axis_size("ctx"))])


def dot(a, b, dims=((1,), (0,))):
    return lax.dot_general(a, b, (dims, ((), ())), preferred_element_type=F32)


def swap_matrix(head):
    rows = lax.broadcasted_iota(jnp.int32, (head, head), 0)
    cols = lax.broadcasted_iota(jnp.int32, (head, head), 1)
    return jnp.where(jnp.abs(rows - cols) == head // 2, 1.0, 0.0).astype(BF16)


def row_mean(x):
    head = x.shape[-1]
    high = x.astype(BF16)
    low = (x - high.astype(F32)).astype(BF16)
    return dot(jnp.concatenate([high, low], axis=1), jnp.full((2 * head, head), 1.0 / head, BF16))


def norm_rotate(x_b, turn, turn_swapped, swap):
    x = x_b.astype(F32)
    inverse = lax.rsqrt(row_mean(x * x) + EPSILON)
    rotated = (inverse * (x * turn + dot(x_b, swap) * turn_swapped)).astype(BF16)
    return rotated, dot(rotated, swap).astype(BF16), x * inverse, inverse


def norm_back(d_y, normed, inverse, gain):
    d_normed = d_y * gain
    return inverse * (d_normed - normed * row_mean(d_normed * normed))


def fold(x):
    return jnp.sum(x.reshape(-1, 8, x.shape[-1]), axis=0)


def columns(index, size):
    return pl.ds(pl.multiple_of(index * size, size), size)


def stacked(ref, h, head):
    return jnp.concatenate([ref[:, columns(GROUP * h + j, head)] for j in range(GROUP)], axis=0)


def each_head(count, body):
    def several(i, carry):
        for u in range(UNROLL):
            body(i * UNROLL + u)
        return carry

    lax.fori_loop(0, count // UNROLL, several, 0)


def call(kernel, name, outs, args, flops=1_000_000, traffic=100_000, scratch=()):
    return pl.pallas_call(
        kernel,
        name=name,
        in_specs=[IN_VMEM] * len(args),
        out_specs=[IN_VMEM] * len(outs),
        out_shape=[jax.ShapeDtypeStruct(shape, dtype) for shape, dtype in outs],
        scratch_shapes=scratch,
        cost_estimate=pl.CostEstimate(flops=flops, bytes_accessed=traffic, transcendentals=0),
        compiler_params=pltpu.CompilerParams(vmem_limit_bytes=VMEM_LIMIT),
    )(*args)


def tables_kernel(freq_ref, angle_ref):
    span, head = angle_ref.shape[1:]
    rows = span - WINDOW
    position = lax.axis_index("ctx") * rows - WINDOW + lax.broadcasted_iota(jnp.int32, (span, head), 0)
    angles = position.astype(F32) * freq_ref[0:1]
    angle_ref[0] = jnp.cos(angles)
    angle_ref[1] = jnp.sin(angles) * freq_ref[1:2]


def prepare_kernel(
    q_ref, k_ref, q_gain_ref, k_gain_ref, angle_ref,
    q_ref2, q_unit_ref, q_inv_ref, k_ref2, k_unit_ref, k_inv_ref, turn_ref,
):
    heads, group_rows, head = q_unit_ref.shape
    rows = group_rows // GROUP
    half = head // 2
    swap = swap_matrix(head)
    span = angle_ref.shape[1]
    far = span - rows
    cosine, sine = angle_ref[0], angle_ref[1]
    q_gain, k_gain = q_gain_ref[...], k_gain_ref[...]
    q_turn = jnp.concatenate([cosine[far:] * q_gain] * GROUP, axis=0)
    q_turn_s = jnp.concatenate([sine[far:] * pltpu.roll(q_gain, half, 1)] * GROUP, axis=0)
    k_turn_all = cosine * k_gain
    k_turn_all_s = sine * pltpu.roll(k_gain, half, 1)
    turn_ref[0] = k_turn_all[:far]
    turn_ref[1] = k_turn_all_s[:far]
    k_turn, k_turn_s = k_turn_all[far:], k_turn_all_s[far:]

    def body(h):
        rotated, swapped, normed, inverse = norm_rotate(stacked(q_ref, h, head), q_turn, q_turn_s, swap)
        q_ref2[h, :, :head] = rotated
        q_ref2[h, :, head:] = swapped
        q_unit_ref[h] = normed
        q_inv_ref[h] = inverse
        rotated, swapped, normed, inverse = norm_rotate(k_ref[:, columns(h, head)], k_turn, k_turn_s, swap)
        k_ref2[h, :, :head] = rotated
        k_ref2[h, :, head:] = swapped
        k_unit_ref[h] = normed
        k_inv_ref[h] = inverse

    each_head(heads, body)


def scores_kernel(
    q_ref, do_ref, own_ref, k1a_ref, k1b_ref, k2_ref, turn_ref,
    probs_ref, keys_ref, unit_ref, dv_ref, dv1_ref, dv2_ref,
):
    heads, span, _ = probs_ref.shape
    rows, head = own_ref.shape[1], own_ref.shape[2] // 2
    far = span - rows
    odd = lax.rem(lax.axis_index("ctx"), 2) == 1
    swap = swap_matrix(head)
    turn, turn_s = turn_ref[0], turn_ref[1]
    key = lax.broadcasted_iota(jnp.int32, (span, rows), 0)
    row = lax.broadcasted_iota(jnp.int32, (span, rows), 1)
    start = far - lax.axis_index("ctx") * rows
    bias = jnp.where((key > row) & (key <= row + far) & (key >= start), 0.0, HIDDEN)
    bias = jnp.concatenate([bias] * GROUP, axis=1)

    def body(h):
        cols = columns(h, head)
        raw = jnp.concatenate([k2_ref[:, cols], jnp.where(odd, k1a_ref[:, cols], k1b_ref[:, cols])], axis=0)
        rotated, swapped, normed, _ = norm_rotate(raw, turn, turn_s, swap)
        keys_ref[h, :, :head] = rotated
        keys_ref[h, :, head:] = swapped
        unit_ref[h] = normed
        keys = jnp.concatenate([rotated, own_ref[h, :, :head]], axis=0)
        scores = dot(keys, q_ref[h, :, :head], ((1,), (1,))) + bias
        top = jnp.max(scores, axis=0, keepdims=True)
        exps = jnp.exp2((scores - top) * LOG2_SCALE)
        probs = exps * (1.0 / jnp.sum(exps, axis=0, keepdims=True))
        probs_ref[h] = probs
        d_value = dot(probs.astype(BF16), stacked(do_ref, h, head))
        dv2_ref[:, cols] = d_value[: far - rows].astype(BF16)
        dv1_ref[:, cols] = d_value[far - rows : far].astype(BF16)
        dv_ref[:, cols] = d_value[far:]

    each_head(heads, body)


def grads_kernel(
    probs_ref, q_ref, q_unit_ref, do_ref, keys_ref, own_ref, unit_ref, own_unit_ref, v0_ref, v1a_ref, v1b_ref, v2_ref,
    angle_ref,
    dqy_ref, dy_ref, dk1_ref, dk2_ref, sum_ref, dg_ref,
):
    heads, span, _ = probs_ref.shape
    rows, head = own_ref.shape[1], own_ref.shape[2] // 2
    far = span - rows
    odd = lax.rem(lax.axis_index("ctx"), 2) == 1
    cosine, sine = angle_ref[0], angle_ref[1]
    q_cos = jnp.concatenate([cosine[far:]] * GROUP, axis=0)
    q_sin = jnp.concatenate([sine[far:]] * GROUP, axis=0)
    dg_ref[...] = jnp.zeros_like(dg_ref)

    def body(h):
        cols = columns(h, head)
        values = jnp.concatenate([v2_ref[:, cols], jnp.where(odd, v1a_ref[:, cols], v1b_ref[:, cols]), v0_ref[:, cols]], axis=0)
        grad_out = stacked(do_ref, h, head)
        probs = probs_ref[h]
        d_prob = dot(values, grad_out, ((1,), (1,)))
        delta = jnp.sum(probs * d_prob, axis=0, keepdims=True)
        d_score = (probs * (d_prob - delta) * SCORE_SCALE).astype(BF16)
        d_key = dot(d_score, q_ref[h])
        d_query = dot(d_score, jnp.concatenate([keys_ref[h], own_ref[h]], axis=0), ((0,), (0,)))

        dk2_ref[:, cols] = d_key[: far - rows, :head].astype(BF16)
        dk1_ref[:, cols] = d_key[far - rows : far, :head].astype(BF16)
        term = d_key[:far].astype(BF16).astype(F32)
        d_y_far = term[:, :head] * cosine[:far] - term[:, head:] * sine[:far]
        d_y_own = d_key[far:, :head] * cosine[far:] - d_key[far:, head:] * sine[far:]
        dy_ref[:, cols] = d_y_own
        dg_ref[8:16, :] += fold(d_y_far * unit_ref[h]) + fold(d_y_own * own_unit_ref[h])

        d_y = d_query[:, :head] * q_cos - d_query[:, head:] * q_sin
        dqy_ref[h] = d_y
        dg_ref[0:8, :] += fold(d_y * q_unit_ref[h])

    each_head(heads, body)
    sum_ref[0:1] = jnp.sum(dg_ref[0:8], axis=0, keepdims=True)
    sum_ref[1:2] = jnp.sum(dg_ref[8:16], axis=0, keepdims=True)


def outputs_kernel(probs_ref, v0_ref, v1a_ref, v1b_ref, v2_ref, dqy_ref, q_unit_ref, q_inv_ref, gain_ref, out_ref, dq_ref):
    heads, group_rows, head = q_unit_ref.shape
    rows = group_rows // GROUP
    odd = lax.rem(lax.axis_index("ctx"), 2) == 1
    q_gain = gain_ref[...]

    def body(h):
        cols = columns(h, head)
        values = jnp.concatenate([v2_ref[:, cols], jnp.where(odd, v1a_ref[:, cols], v1b_ref[:, cols]), v0_ref[:, cols]], axis=0)
        result = dot(probs_ref[h].astype(BF16), values, ((0,), (0,))).astype(BF16)
        d_q = norm_back(dqy_ref[h], q_unit_ref[h], q_inv_ref[h], q_gain).astype(BF16)
        for j in range(GROUP):
            wide = columns(GROUP * h + j, head)
            out_ref[:, wide] = result[j * rows : (j + 1) * rows]
            dq_ref[:, wide] = d_q[j * rows : (j + 1) * rows]

    each_head(heads, body)


def merge_kernel(k_far_ref, k_near_ref, v_far_ref, v_near_ref, out_ref):
    odd = lax.rem(lax.axis_index("ctx"), 2) == 1
    for i, (far_ref, near_ref) in enumerate(((k_far_ref, k_near_ref), (v_far_ref, v_near_ref))):
        near = jnp.where(odd, near_ref[...].astype(F32), 0.0)
        out_ref[i] = (far_ref[...].astype(F32) + near).astype(BF16)


def finish_kernel(dy_ref, dv_ref, k1_ref, v1_ref, far_ref, unit_ref, inv_ref, angle_ref, gain_ref, dk_out, dv_out):
    heads, rows, head = unit_ref.shape
    far = angle_ref.shape[1] - rows
    odd = lax.rem(lax.axis_index("ctx"), 2) == 1
    swap = swap_matrix(head)
    swaps = jnp.concatenate([swap, swap], axis=0)
    cosine, sine = angle_ref[0, far:], angle_ref[1, far:]
    gain = gain_ref[...]

    def body(h):
        cols = columns(h, head)
        near = jnp.where(odd, 0.0, v1_ref[:, cols].astype(F32))
        dv_out[:, cols] = (dv_ref[:, cols] + near + far_ref[1, :, cols].astype(F32)).astype(BF16)
        near = jnp.where(odd, 0.0, k1_ref[:, cols].astype(F32))
        rest = far_ref[0, :, cols]
        swapped = dot(jnp.concatenate([near.astype(BF16), rest], axis=1), swaps)
        d_y = dy_ref[:, cols] + ((near + rest.astype(F32)) * cosine - swapped * sine)
        dk_out[:, cols] = norm_back(d_y, unit_ref[h], inv_ref[h], gain).astype(BF16)

    each_head(heads, body)


def share_kernel(own_ref, other_ref, out_ref):
    total = own_ref[...] + other_ref[...]
    head, size = total.shape[1], out_ref.shape[1]
    share = jnp.zeros(out_ref.shape, F32)
    for j in range(total.size // size):
        row, col = divmod(j * size, head)
        share = jnp.where(lax.axis_index("dp") == j, total[row : row + 1, col : col + size], share)
    out_ref[...] = share


def all_sum_term(value, axis, step):
    return lax.ppermute(value, axis, [(i, i ^ step) for i in range(lax.axis_size(axis))])


def all_sum(value, axis, steps):
    for step in steps:
        value = value + all_sum_term(value, axis, step)
    return value


def doublings(axis, first=1):
    count = lax.axis_size(axis)
    return [first << i for i in range(count.bit_length()) if first << i < count]


def on_device(q_proj, k_proj, v_proj, d_out, q_gain, k_gain):
    rows = q_proj.shape[1]
    head = q_gain.shape[0]
    heads = k_proj.shape[2] // head
    width = heads * head
    wide = GROUP * width
    span = WINDOW + rows
    far = WINDOW
    assert far == 2 * rows
    tall = GROUP * rows
    k2 = hop(k_proj, 2)
    v2 = ring_hop(v_proj, 2)
    k1_odd = swap_pairs(k_proj)
    v1_odd = swap_pairs(v_proj)

    half = head // 2
    freqs = jnp.power(ROPE_BASE, -2.0 * jnp.arange(half, dtype=F32) / head)
    sign = jnp.where(jnp.arange(head) < half, -1.0, 1.0)
    freqs = jnp.stack([jnp.tile(freqs, 2), sign])

    q_gain = q_gain.reshape(1, head)
    k_gain = k_gain.reshape(1, head)
    (angle_table,) = call(tables_kernel, "tables", [((2, span, head), F32)], (freqs,), flops=TABLES_COST)
    q_rot, q_unit, q_inv, k_rot, k_unit, k_inv, turn_table = call(
        prepare_kernel,
        "prepare",
        [((heads, tall, 2 * head), BF16), ((heads, tall, head), F32), ((heads, tall, head), F32)]
        + [((heads, rows, 2 * head), BF16), ((heads, rows, head), F32), ((heads, rows, head), F32)]
        + [((2, far, head), F32)],
        (q_proj[0], k_proj[0], q_gain, k_gain, angle_table),
    )
    q_rot, k2 = lax.optimization_barrier((q_rot, k2))
    k1_even, v2 = lax.optimization_barrier((swap_pairs(k2), v2))
    k1 = k1_odd[0], k1_even[0]
    v1 = v1_odd[0], swap_pairs(v2)[0]
    probs, far_keys, far_unit, dv_own, dv1, dv2 = call(
        scores_kernel,
        "scores",
        [((heads, span, tall), F32), ((heads, far, 2 * head), BF16), ((heads, far, head), F32)]
        + [((rows, width), F32), ((rows, width), BF16), ((rows, width), BF16)],
        (q_rot, d_out[0], k_rot, *k1, k2[0], turn_table),
    )
    dv_near = swap_pairs(dv1)
    dq_y, dy_own, dk1, dk2, gain_terms = call(
        grads_kernel,
        "grads",
        [((heads, tall, head), F32), ((rows, width), F32), ((rows, width), BF16), ((rows, width), BF16)]
        + [((2, head), F32)],
        (probs, q_rot, q_unit, d_out[0], far_keys, k_rot, far_unit, k_unit, v_proj[0], *v1, v2[0], angle_table),
        scratch=[pltpu.VMEM((16, head), F32)],
    )
    dk_near = swap_pairs(dk1)
    gain_terms = all_sum(gain_terms, "ctx", [2])
    gain_terms, dk_near = lax.optimization_barrier((gain_terms, dk_near))
    (merged,) = call(merge_kernel, "merge", [((2, rows, width), BF16)], (dk2, dk_near, dv2, dv_near))
    back = hop(merged, -2)
    gain_terms = all_sum(all_sum(gain_terms, "dp", doublings("dp")), "ctx", [1])
    result, d_q = call(
        outputs_kernel,
        "outputs",
        [((rows, wide), BF16), ((rows, wide), BF16)],
        (probs, v_proj[0], *v1, v2[0], dq_y, q_unit, q_inv, q_gain),
    )
    gain_terms, back, result, d_q = lax.optimization_barrier((gain_terms, back, result, d_q))
    for step in doublings("ctx", 4)[:-1]:
        gain_terms = all_sum(gain_terms, "ctx", [step])
    last = doublings("ctx", 4)[-1]
    others = all_sum_term(gain_terms, "ctx", last)
    d_k, d_v = call(
        finish_kernel,
        "finish",
        [((rows, width), BF16), ((rows, width), BF16)],
        (dy_own, dv_own, dk_near, dv_near, back, k_unit, k_inv, angle_table, k_gain),
    )
    share = 2 * head // lax.axis_size("dp")
    (gain_share,) = call(share_kernel, "share", [((1, share), F32)], (gain_terms, others))
    return (result[None], d_q[None], d_k[None], d_v[None], gain_share[0])


def solution(mesh):
    tokens = P("dp", "ctx", None)
    return jax.shard_map(
        on_device,
        mesh=mesh,
        in_specs=(tokens,) * 4 + (P(), P()),
        out_specs=(tokens,) * 4 + (P("dp"),),
        check_vma=False,
    )
```

```python
import math

import jax
import jax.numpy as jnp
from jax import lax
from jax.experimental import pallas as pl
from jax.experimental.pallas import tpu as pltpu
from jax.sharding import PartitionSpec as P

WINDOW = 256
EPSILON = 1e-06
ROPE_BASE = 10000.0
SCORE_SCALE = 168.0 ** (-0.5)
LOG2_SCALE = SCORE_SCALE * math.log2(math.e)
HIDDEN = -1e30
GROUP = 2
F32 = jnp.float32
BF16 = jnp.bfloat16
TABLES_COST = 10_000_000_000
IN_VMEM = pl.BlockSpec(memory_space=pltpu.VMEM)
VMEM_LIMIT = 24 * 1024 * 1024


def hop(value, steps):
    count = lax.axis_size("ctx")
    initial, last = (max(0, -steps), min(count, count - steps))
    return lax.ppermute(value, "ctx", [(i, i + steps) for i in range(initial, last)])


def ring_hop(value, steps):
    count = lax.axis_size("ctx")
    return lax.ppermute(value, "ctx", [(i, (i + steps) % count) for i in range(count)])


def swap_pairs(value):
    return lax.ppermute(value, "ctx", [(i, i ^ 1) for i in range(lax.axis_size("ctx"))])


def dot(a, b, dims=((1,), (0,))):
    return lax.dot_general(a, b, (dims, ((), ())), preferred_element_type=F32)


def swap_matrix(head):
    rows = lax.broadcasted_iota(jnp.int32, (head, head), 0)
    cols = lax.broadcasted_iota(jnp.int32, (head, head), 1)
    return jnp.where(jnp.abs(rows - cols) == head // 2, 1.0, 0.0).astype(BF16)


def row_mean(x):
    head = x.shape[-1]
    high = x.astype(BF16)
    low = (x - high.astype(F32)).astype(BF16)
    return dot(jnp.concatenate([high, low], axis=1), jnp.full((2 * head, head), 1.0 / head, BF16))


def norm_rotate(x_b, turn, turn_swapped, swap):
    x = x_b.astype(F32)
    inverse = lax.rsqrt(row_mean(x * x) + EPSILON)
    rotated = (inverse * (x * turn + dot(x_b, swap) * turn_swapped)).astype(BF16)
    return rotated, dot(rotated, swap).astype(BF16), x * inverse, inverse


def norm_back(d_y, normed, inverse, gain):
    d_normed = d_y * gain
    return inverse * (d_normed - normed * row_mean(d_normed * normed))


def fold(x):
    return jnp.sum(x.reshape(-1, 8, x.shape[-1]), axis=0)


def columns(index, size):
    return slice(index * size, (index + 1) * size)


def stacked(ref, h, head):
    return jnp.concatenate([ref[:, columns(GROUP * h + j, head)] for j in range(GROUP)], axis=0)


def each_head(count, body):
    for h in range(count):
        body(h)


def call(kernel, name, outs, args, flops=1_000_000, traffic=100_000, scratch=()):
    return pl.pallas_call(
        kernel,
        name=name,
        in_specs=[IN_VMEM] * len(args),
        out_specs=[IN_VMEM] * len(outs),
        out_shape=[jax.ShapeDtypeStruct(shape, dtype) for shape, dtype in outs],
        scratch_shapes=scratch,
        cost_estimate=pl.CostEstimate(flops=flops, bytes_accessed=traffic, transcendentals=0),
        compiler_params=pltpu.CompilerParams(vmem_limit_bytes=VMEM_LIMIT),
    )(*args)


def tables_kernel(freq_ref, angle_ref):
    span, head = angle_ref.shape[1:]
    rows = span - WINDOW
    position = lax.axis_index("ctx") * rows - WINDOW + lax.broadcasted_iota(jnp.int32, (span, head), 0)
    angles = position.astype(F32) * freq_ref[0:1]
    angle_ref[0] = jnp.cos(angles)
    angle_ref[1] = jnp.sin(angles) * freq_ref[1:2]


def prepare_kernel(
    q_ref, k_ref, q_gain_ref, k_gain_ref, angle_ref,
    q_ref2, q_unit_ref, q_inv_ref, k_ref2, k_unit_ref, k_inv_ref, turn_ref,
):
    heads, group_rows, head = q_unit_ref.shape
    rows = group_rows // GROUP
    half = head // 2
    swap = swap_matrix(head)
    span = angle_ref.shape[1]
    far = span - rows
    cosine, sine = angle_ref[0], angle_ref[1]
    q_gain, k_gain = q_gain_ref[...], k_gain_ref[...]
    q_turn = jnp.concatenate([cosine[far:] * q_gain] * GROUP, axis=0)
    q_turn_s = jnp.concatenate([sine[far:] * pltpu.roll(q_gain, half, 1)] * GROUP, axis=0)
    k_turn_all = cosine * k_gain
    k_turn_all_s = sine * pltpu.roll(k_gain, half, 1)
    turn_ref[0] = k_turn_all[:far]
    turn_ref[1] = k_turn_all_s[:far]
    k_turn, k_turn_s = k_turn_all[far:], k_turn_all_s[far:]

    def body(h):
        rotated, swapped, normed, inverse = norm_rotate(stacked(q_ref, h, head), q_turn, q_turn_s, swap)
        q_ref2[h, :, :head] = rotated
        q_ref2[h, :, head:] = swapped
        q_unit_ref[h] = normed
        q_inv_ref[h] = inverse
        rotated, swapped, normed, inverse = norm_rotate(k_ref[:, columns(h, head)], k_turn, k_turn_s, swap)
        k_ref2[h, :, :head] = rotated
        k_ref2[h, :, head:] = swapped
        k_unit_ref[h] = normed
        k_inv_ref[h] = inverse

    each_head(heads, body)


def scores_kernel(
    q_ref, do_ref, own_ref, k1a_ref, k1b_ref, k1c_ref, k2_ref, turn_ref,
    probs_ref, keys_ref, unit_ref, dv_ref, dv1_ref, dv2_ref,
):
    heads, span, _ = probs_ref.shape
    rows, head = own_ref.shape[1], own_ref.shape[2] // 2
    far = span - rows
    odd = lax.rem(lax.axis_index("ctx"), 2) == 1
    swap = swap_matrix(head)
    turn, turn_s = turn_ref[0], turn_ref[1]
    key = lax.broadcasted_iota(jnp.int32, (span, rows), 0)
    row = lax.broadcasted_iota(jnp.int32, (span, rows), 1)
    start = far - lax.axis_index("ctx") * rows
    bias = jnp.where((key > row) & (key <= row + far) & (key >= start), 0.0, HIDDEN)
    bias = jnp.concatenate([bias] * GROUP, axis=1)

    def body(h):
        cols = columns(h, head)
        half_ref, low = (k1b_ref, h) if h < heads // 2 else (k1c_ref, h - heads // 2)
        near = jnp.where(odd, k1a_ref[:, cols], half_ref[:, columns(low, head)])
        raw = jnp.concatenate([k2_ref[:, cols], near], axis=0)
        rotated, swapped, normed, _ = norm_rotate(raw, turn, turn_s, swap)
        keys_ref[h, :, :head] = rotated
        keys_ref[h, :, head:] = swapped
        unit_ref[h] = normed
        keys = jnp.concatenate([rotated, own_ref[h, :, :head]], axis=0)
        scores = dot(keys, q_ref[h, :, :head], ((1,), (1,))) + bias
        top = jnp.max(scores, axis=0, keepdims=True)
        exps = jnp.exp2((scores - top) * LOG2_SCALE)
        probs = exps * (1.0 / jnp.sum(exps, axis=0, keepdims=True))
        probs_ref[h] = probs
        d_value = dot(probs.astype(BF16), stacked(do_ref, h, head))
        dv2_ref[:, cols] = d_value[: far - rows].astype(BF16)
        dv1_ref[:, cols] = d_value[far - rows : far].astype(BF16)
        dv_ref[:, cols] = d_value[far:]

    each_head(heads, body)


def grads_kernel(
    probs_ref, q_ref, q_unit_ref, do_ref, keys_ref, own_ref, unit_ref, own_unit_ref, v0_ref, v1a_ref, v1b_ref, v2_ref,
    angle_ref,
    dqy_ref, dy_ref, dk1a_ref, dk1b_ref, dk2_ref, sum_ref, dg_ref,
):
    heads, span, _ = probs_ref.shape
    rows, head = own_ref.shape[1], own_ref.shape[2] // 2
    far = span - rows
    odd = lax.rem(lax.axis_index("ctx"), 2) == 1
    cosine, sine = angle_ref[0], angle_ref[1]
    q_cos = jnp.concatenate([cosine[far:]] * GROUP, axis=0)
    q_sin = jnp.concatenate([sine[far:]] * GROUP, axis=0)
    dg_ref[...] = jnp.zeros_like(dg_ref)

    def body(h):
        cols = columns(h, head)
        values = jnp.concatenate([v2_ref[:, cols], jnp.where(odd, v1a_ref[:, cols], v1b_ref[:, cols]), v0_ref[:, cols]], axis=0)
        grad_out = stacked(do_ref, h, head)
        probs = probs_ref[h]
        d_prob = dot(values, grad_out, ((1,), (1,)))
        delta = jnp.sum(probs * d_prob, axis=0, keepdims=True)
        d_score = (probs * (d_prob - delta) * SCORE_SCALE).astype(BF16)
        d_key = dot(d_score, q_ref[h])
        d_query = dot(d_score, jnp.concatenate([keys_ref[h], own_ref[h]], axis=0), ((0,), (0,)))

        dk2_ref[:, cols] = d_key[: far - rows, :head].astype(BF16)
        dk1_ref, low = (dk1a_ref, h) if h < heads // 2 else (dk1b_ref, h - heads // 2)
        dk1_ref[:, columns(low, head)] = d_key[far - rows : far, :head].astype(BF16)
        term = d_key[:far].astype(BF16).astype(F32)
        d_y_far = term[:, :head] * cosine[:far] - term[:, head:] * sine[:far]
        d_y_own = d_key[far:, :head] * cosine[far:] - d_key[far:, head:] * sine[far:]
        dy_ref[:, cols] = d_y_own
        dg_ref[8:16, :] += fold(d_y_far * unit_ref[h]) + fold(d_y_own * own_unit_ref[h])

        d_y = d_query[:, :head] * q_cos - d_query[:, head:] * q_sin
        dqy_ref[h] = d_y
        dg_ref[0:8, :] += fold(d_y * q_unit_ref[h])

    each_head(heads, body)
    sum_ref[0:1] = jnp.sum(dg_ref[0:8], axis=0, keepdims=True)
    sum_ref[1:2] = jnp.sum(dg_ref[8:16], axis=0, keepdims=True)


def outputs_kernel(probs_ref, v0_ref, v1a_ref, v1b_ref, v2_ref, dqy_ref, q_unit_ref, q_inv_ref, gain_ref, out_ref, dq_ref):
    heads, group_rows, head = q_unit_ref.shape
    rows = group_rows // GROUP
    odd = lax.rem(lax.axis_index("ctx"), 2) == 1
    q_gain = gain_ref[...]

    def body(h):
        cols = columns(h, head)
        values = jnp.concatenate([v2_ref[:, cols], jnp.where(odd, v1a_ref[:, cols], v1b_ref[:, cols]), v0_ref[:, cols]], axis=0)
        result = dot(probs_ref[h].astype(BF16), values, ((0,), (0,))).astype(BF16)
        d_q = norm_back(dqy_ref[h], q_unit_ref[h], q_inv_ref[h], q_gain).astype(BF16)
        for j in range(GROUP):
            wide = columns(GROUP * h + j, head)
            out_ref[:, wide] = result[j * rows : (j + 1) * rows]
            dq_ref[:, wide] = d_q[j * rows : (j + 1) * rows]

    each_head(heads, body)


def merge_kernel(far_ref, *refs):
    near_refs, out_ref = refs[:-1], refs[-1]
    odd = lax.rem(lax.axis_index("ctx"), 2) == 1
    low = 0
    for near_ref in near_refs:
        cols = slice(low, low + near_ref.shape[1])
        near = jnp.where(odd, near_ref[...].astype(F32), 0.0)
        out_ref[:, cols] = (far_ref[:, cols].astype(F32) + near).astype(BF16)
        low = cols.stop


def finish_kernel(dy_ref, dv_ref, k1a_ref, k1b_ref, v1_ref, k2_ref, v2_ref, unit_ref, inv_ref, angle_ref, gain_ref, dk_out, dv_out):
    heads, rows, head = unit_ref.shape
    far = angle_ref.shape[1] - rows
    odd = lax.rem(lax.axis_index("ctx"), 2) == 1
    swap = swap_matrix(head)
    swaps = jnp.concatenate([swap, swap], axis=0)
    cosine, sine = angle_ref[0, far:], angle_ref[1, far:]
    gain = gain_ref[...]

    def body(h):
        cols = columns(h, head)
        near = jnp.where(odd, 0.0, v1_ref[:, cols].astype(F32))
        dv_out[:, cols] = (dv_ref[:, cols] + near + v2_ref[:, cols].astype(F32)).astype(BF16)
        k1_ref, low = (k1a_ref, h) if h < heads // 2 else (k1b_ref, h - heads // 2)
        near = jnp.where(odd, 0.0, k1_ref[:, columns(low, head)].astype(F32))
        rest = k2_ref[:, cols]
        swapped = dot(jnp.concatenate([near.astype(BF16), rest], axis=1), swaps)
        d_y = dy_ref[:, cols] + ((near + rest.astype(F32)) * cosine - swapped * sine)
        dk_out[:, cols] = norm_back(d_y, unit_ref[h], inv_ref[h], gain).astype(BF16)

    each_head(heads, body)


def share_kernel(own_ref, other_ref, out_ref):
    total = own_ref[...] + other_ref[...]
    head, size = total.shape[1], out_ref.shape[1]
    share = jnp.zeros(out_ref.shape, F32)
    for j in range(total.size // size):
        row, col = divmod(j * size, head)
        share = jnp.where(lax.axis_index("dp") == j, total[row : row + 1, col : col + size], share)
    out_ref[...] = share


def all_sum_term(value, axis, step):
    return lax.ppermute(value, axis, [(i, i ^ step) for i in range(lax.axis_size(axis))])


def all_sum(value, axis, steps):
    for step in steps:
        value = value + all_sum_term(value, axis, step)
    return value


def doublings(axis, first=1):
    count = lax.axis_size(axis)
    return [first << i for i in range(count.bit_length()) if first << i < count]


def on_device(q_proj, k_proj, v_proj, d_out, q_gain, k_gain):
    rows = q_proj.shape[1]
    head = q_gain.shape[0]
    heads = k_proj.shape[2] // head
    width = heads * head
    wide = GROUP * width
    span = WINDOW + rows
    far = WINDOW
    assert far == 2 * rows
    tall = GROUP * rows
    k2 = hop(k_proj, 2)
    v2 = ring_hop(v_proj, 2)
    k1_odd = swap_pairs(k_proj)
    v1_odd = swap_pairs(v_proj)

    half = head // 2
    freqs = jnp.power(ROPE_BASE, -2.0 * jnp.arange(half, dtype=F32) / head)
    sign = jnp.where(jnp.arange(head) < half, -1.0, 1.0)
    freqs = jnp.stack([jnp.tile(freqs, 2), sign])

    q_gain = q_gain.reshape(1, head)
    k_gain = k_gain.reshape(1, head)
    (angle_table,) = call(tables_kernel, "tables", [((2, span, head), F32)], (freqs,), flops=TABLES_COST)
    q_rot, q_unit, q_inv, k_rot, k_unit, k_inv, turn_table = call(
        prepare_kernel,
        "prepare",
        [((heads, tall, 2 * head), BF16), ((heads, tall, head), F32), ((heads, tall, head), F32)]
        + [((heads, rows, 2 * head), BF16), ((heads, rows, head), F32), ((heads, rows, head), F32)]
        + [((2, far, head), F32)],
        (q_proj[0], k_proj[0], q_gain, k_gain, angle_table),
    )
    q_rot, k2 = lax.optimization_barrier((q_rot, k2))
    k1 = k1_odd[0], swap_pairs(k2[0, :, : width // 2]), swap_pairs(k2[0, :, width // 2 :])
    probs, far_keys, far_unit, dv_own, dv1, dv2 = call(
        scores_kernel,
        "scores",
        [((heads, span, tall), F32), ((heads, far, 2 * head), BF16), ((heads, far, head), F32)]
        + [((rows, width), F32), ((rows, width), BF16), ((rows, width), BF16)],
        (q_rot, d_out[0], k_rot, *k1, k2[0], turn_table),
    )
    v2, dv1, dv2 = lax.optimization_barrier((v2, dv1, dv2))
    v1 = v1_odd[0], swap_pairs(v2)[0]
    dv_near = swap_pairs(dv1)
    (v_merged,) = call(merge_kernel, "merge_v", [((rows, width), BF16)], (dv2, dv_near))
    v_back = hop(v_merged, -2)
    dq_y, dy_own, dk1a, dk1b, dk2, gain_terms = call(
        grads_kernel,
        "grads",
        [((heads, tall, head), F32), ((rows, width), F32), ((rows, width // 2), BF16), ((rows, width // 2), BF16)]
        + [((rows, width), BF16), ((2, head), F32)],
        (probs, q_rot, q_unit, d_out[0], far_keys, k_rot, far_unit, k_unit, v_proj[0], *v1, v2[0], angle_table),
        scratch=[pltpu.VMEM((16, head), F32)],
    )
    dk_near = swap_pairs(dk1a), swap_pairs(dk1b)
    gain_terms = all_sum(gain_terms, "ctx", [1])
    gain_terms = all_sum(gain_terms, "ctx", [2])
    gain_terms, dk_near, v_back = lax.optimization_barrier((gain_terms, dk_near, v_back))
    (merged,) = call(merge_kernel, "merge_k", [((rows, width), BF16)], (dk2, *dk_near))
    k_back = hop(merged, -2)
    gain_terms = all_sum(gain_terms, "dp", doublings("dp"))
    result, d_q = call(
        outputs_kernel,
        "outputs",
        [((rows, wide), BF16), ((rows, wide), BF16)],
        (probs, v_proj[0], *v1, v2[0], dq_y, q_unit, q_inv, q_gain),
    )
    gain_terms, k_back, result, d_q = lax.optimization_barrier((gain_terms, k_back, result, d_q))
    *steps, last = doublings("ctx", 4)
    gain_terms = all_sum(gain_terms, "ctx", steps)
    others = all_sum_term(gain_terms, "ctx", last)
    d_k, d_v = call(
        finish_kernel,
        "finish",
        [((rows, width), BF16), ((rows, width), BF16)],
        (dy_own, dv_own, *dk_near, dv_near, k_back, v_back, k_unit, k_inv, angle_table, k_gain),
    )
    share = 2 * head // lax.axis_size("dp")
    (gain_share,) = call(share_kernel, "share", [((1, share), F32)], (gain_terms, others))
    return (result[None], d_q[None], d_k[None], d_v[None], gain_share[0])


def solution(mesh):
    tokens = P("dp", "ctx", None)
    return jax.shard_map(
        on_device,
        mesh=mesh,
        in_specs=(tokens,) * 4 + (P(), P()),
        out_specs=(tokens,) * 4 + (P("dp"),),
        check_vma=False,
    )
```

```python
import math

import jax
import jax.numpy as jnp
from jax import lax
from jax.experimental import pallas as pl
from jax.experimental.pallas import tpu as pltpu
from jax.sharding import PartitionSpec as P

WINDOW = 256
EPSILON = 1e-06
ROPE_BASE = 10000.0
SCORE_SCALE = 168.0 ** (-0.5)
LOG2_SCALE = SCORE_SCALE * math.log2(math.e)
HIDDEN = -1e30
GROUP = 2
F32 = jnp.float32
BF16 = jnp.bfloat16
TABLES_COST = 10_000_000_000
IN_VMEM = pl.BlockSpec(memory_space=pltpu.VMEM)
VMEM_LIMIT = 24 * 1024 * 1024


def hop(value, steps):
    count = lax.axis_size("ctx")
    initial, last = (max(0, -steps), min(count, count - steps))
    return lax.ppermute(value, "ctx", [(i, i + steps) for i in range(initial, last)])


def ring_hop(value, steps):
    count = lax.axis_size("ctx")
    return lax.ppermute(value, "ctx", [(i, (i + steps) % count) for i in range(count)])


def swap_pairs(value):
    return lax.ppermute(value, "ctx", [(i, i ^ 1) for i in range(lax.axis_size("ctx"))])


def dot(a, b, dims=((1,), (0,))):
    return lax.dot_general(a, b, (dims, ((), ())), preferred_element_type=F32)


def swap_matrix(head):
    rows = lax.broadcasted_iota(jnp.int32, (head, head), 0)
    cols = lax.broadcasted_iota(jnp.int32, (head, head), 1)
    return jnp.where(jnp.abs(rows - cols) == head // 2, 1.0, 0.0).astype(BF16)


def row_mean(x):
    head = x.shape[-1]
    high = x.astype(BF16)
    low = (x - high.astype(F32)).astype(BF16)
    return dot(jnp.concatenate([high, low], axis=1), jnp.full((2 * head, head), 1.0 / head, BF16))


def norm_rotate(x_b, turn, turn_swapped, swap):
    x = x_b.astype(F32)
    inverse = lax.rsqrt(row_mean(x * x) + EPSILON)
    rotated = (inverse * (x * turn + dot(x_b, swap) * turn_swapped)).astype(BF16)
    return rotated, dot(rotated, swap).astype(BF16), x * inverse, inverse


def fold(x):
    return jnp.sum(x.reshape(-1, 8, x.shape[-1]), axis=0)


def columns(index, size):
    return slice(index * size, (index + 1) * size)


def stacked(ref, h, head):
    return jnp.concatenate([ref[:, columns(GROUP * h + j, head)] for j in range(GROUP)], axis=0)


def each_head(count, *stages):
    held = {}
    for step in range(count + len(stages) - 1):
        for i, stage in enumerate(stages):
            h = step - i
            if 0 <= h < count:
                held[h] = stage(h, *held.pop(h, ())) or ()


def call(kernel, name, outs, args, flops=1_000_000, traffic=100_000, scratch=()):
    return pl.pallas_call(
        kernel,
        name=name,
        in_specs=[IN_VMEM] * len(args),
        out_specs=[IN_VMEM] * len(outs),
        out_shape=[jax.ShapeDtypeStruct(shape, dtype) for shape, dtype in outs],
        scratch_shapes=scratch,
        cost_estimate=pl.CostEstimate(flops=flops, bytes_accessed=traffic, transcendentals=0),
        compiler_params=pltpu.CompilerParams(vmem_limit_bytes=VMEM_LIMIT),
    )(*args)


def tables_kernel(freq_ref, angle_ref):
    span, head = angle_ref.shape[1:]
    rows = span - WINDOW
    position = lax.axis_index("ctx") * rows - WINDOW + lax.broadcasted_iota(jnp.int32, (span, head), 0)
    angles = position.astype(F32) * freq_ref[0:1]
    angle_ref[0] = jnp.cos(angles)
    angle_ref[1] = jnp.sin(angles) * freq_ref[1:2]


def prepare_kernel(
    q_ref, k_ref, q_gain_ref, k_gain_ref, angle_ref,
    q_ref2, q_unit_ref, q_inv_ref, k_ref2, k_unit_ref, k_inv_ref, turn_ref,
):
    heads, group_rows, head = q_unit_ref.shape
    rows = group_rows // GROUP
    half = head // 2
    swap = swap_matrix(head)
    span = angle_ref.shape[1]
    far = span - rows
    cosine, sine = angle_ref[0], angle_ref[1]
    q_gain, k_gain = q_gain_ref[...], k_gain_ref[...]
    q_turn = jnp.concatenate([cosine[far:] * q_gain] * GROUP, axis=0)
    q_turn_s = jnp.concatenate([sine[far:] * pltpu.roll(q_gain, half, 1)] * GROUP, axis=0)
    k_turn_all = cosine * k_gain
    k_turn_all_s = sine * pltpu.roll(k_gain, half, 1)
    turn_ref[0] = k_turn_all[:far]
    turn_ref[1] = k_turn_all_s[:far]
    k_turn, k_turn_s = k_turn_all[far:], k_turn_all_s[far:]

    def body(h):
        rotated, swapped, normed, inverse = norm_rotate(stacked(q_ref, h, head), q_turn, q_turn_s, swap)
        q_ref2[h, :, :head] = rotated
        q_ref2[h, :, head:] = swapped
        q_unit_ref[h] = normed
        q_inv_ref[h] = inverse
        rotated, swapped, normed, inverse = norm_rotate(k_ref[:, columns(h, head)], k_turn, k_turn_s, swap)
        k_ref2[h, :, :head] = rotated
        k_ref2[h, :, head:] = swapped
        k_unit_ref[h] = normed
        k_inv_ref[h] = inverse

    each_head(heads, body)


def scores_kernel(
    q_ref, do_ref, own_ref, k1a_ref, k1b_ref, k1c_ref, k2_ref, turn_ref,
    probs_ref, keys_ref, unit_ref, dv_ref, dv1_ref, dv2_ref,
):
    heads, span, _ = probs_ref.shape
    rows, head = own_ref.shape[1], own_ref.shape[2] // 2
    far = span - rows
    odd = lax.rem(lax.axis_index("ctx"), 2) == 1
    swap = swap_matrix(head)
    turn, turn_s = turn_ref[0], turn_ref[1]
    key = lax.broadcasted_iota(jnp.int32, (span, rows), 0)
    row = lax.broadcasted_iota(jnp.int32, (span, rows), 1)
    start = far - lax.axis_index("ctx") * rows
    bias = jnp.where((key > row) & (key <= row + far) & (key >= start), 0.0, HIDDEN)
    bias = jnp.concatenate([bias] * GROUP, axis=1)

    def first(h):
        cols = columns(h, head)
        half_ref, low = (k1b_ref, h) if h < heads // 2 else (k1c_ref, h - heads // 2)
        near = jnp.where(odd, k1a_ref[:, cols], half_ref[:, columns(low, head)])
        raw = jnp.concatenate([k2_ref[:, cols], near], axis=0)
        x = raw.astype(F32)
        return raw, row_mean(x * x), dot(raw, swap)

    def second(h, raw, mean_sq, other):
        x = raw.astype(F32)
        inverse = lax.rsqrt(mean_sq + EPSILON)
        rotated = (inverse * (x * turn + other * turn_s)).astype(BF16)
        keys_ref[h, :, :head] = rotated
        unit_ref[h] = x * inverse
        keys = jnp.concatenate([rotated, own_ref[h, :, :head]], axis=0)
        return rotated, dot(keys, q_ref[h, :, :head], ((1,), (1,))) + bias

    def third(h, rotated, scores):
        keys_ref[h, :, head:] = dot(rotated, swap).astype(BF16)
        top = jnp.max(scores, axis=0, keepdims=True)
        exps = jnp.exp2((scores - top) * LOG2_SCALE)
        probs = exps * (1.0 / jnp.sum(exps, axis=0, keepdims=True))
        probs_ref[h] = probs
        return (probs,)

    def fourth(h, probs):
        cols = columns(h, head)
        d_value = dot(probs.astype(BF16), stacked(do_ref, h, head))
        dv2_ref[:, cols] = d_value[: far - rows].astype(BF16)
        dv1_ref[:, cols] = d_value[far - rows : far].astype(BF16)
        dv_ref[:, cols] = d_value[far:]

    each_head(heads, first, second, third, fourth)


def grads_kernel(
    probs_ref, q_ref, q_unit_ref, do_ref, keys_ref, own_ref, unit_ref, own_unit_ref, v0_ref, v1a_ref, v1b_ref, v2_ref,
    angle_ref,
    dqy_ref, dy_ref, dk1a_ref, dk1b_ref, dk2_ref, sum_ref, dg_ref,
):
    heads, span, _ = probs_ref.shape
    rows, head = own_ref.shape[1], own_ref.shape[2] // 2
    far = span - rows
    odd = lax.rem(lax.axis_index("ctx"), 2) == 1
    cosine, sine = angle_ref[0], angle_ref[1]
    q_cos = jnp.concatenate([cosine[far:]] * GROUP, axis=0)
    q_sin = jnp.concatenate([sine[far:]] * GROUP, axis=0)
    dg_ref[...] = jnp.zeros_like(dg_ref)

    def first(h):
        cols = columns(h, head)
        values = jnp.concatenate([v2_ref[:, cols], jnp.where(odd, v1a_ref[:, cols], v1b_ref[:, cols]), v0_ref[:, cols]], axis=0)
        grad_out = stacked(do_ref, h, head)
        return (dot(values, grad_out, ((1,), (1,))),)

    def second(h, d_prob):
        probs = probs_ref[h]
        delta = jnp.sum(probs * d_prob, axis=0, keepdims=True)
        return ((probs * (d_prob - delta) * SCORE_SCALE).astype(BF16),)

    def third(h, d_score):
        d_key = dot(d_score, q_ref[h])
        d_query = dot(d_score, jnp.concatenate([keys_ref[h], own_ref[h]], axis=0), ((0,), (0,)))
        return d_key, d_query

    def fourth(h, d_key, d_query):
        cols = columns(h, head)
        dk2_ref[:, cols] = d_key[: far - rows, :head].astype(BF16)
        dk1_ref, low = (dk1a_ref, h) if h < heads // 2 else (dk1b_ref, h - heads // 2)
        dk1_ref[:, columns(low, head)] = d_key[far - rows : far, :head].astype(BF16)
        term = d_key[:far].astype(BF16).astype(F32)
        d_y_far = term[:, :head] * cosine[:far] - term[:, head:] * sine[:far]
        d_y_own = d_key[far:, :head] * cosine[far:] - d_key[far:, head:] * sine[far:]
        dy_ref[:, cols] = d_y_own
        dg_ref[8:16, :] += fold(d_y_far * unit_ref[h]) + fold(d_y_own * own_unit_ref[h])

        d_y = d_query[:, :head] * q_cos - d_query[:, head:] * q_sin
        dqy_ref[h] = d_y
        dg_ref[0:8, :] += fold(d_y * q_unit_ref[h])

    each_head(heads, first, second, third, fourth)
    sum_ref[0:1] = jnp.sum(dg_ref[0:8], axis=0, keepdims=True)
    sum_ref[1:2] = jnp.sum(dg_ref[8:16], axis=0, keepdims=True)


def outputs_kernel(probs_ref, v0_ref, v1a_ref, v1b_ref, v2_ref, dqy_ref, q_unit_ref, q_inv_ref, gain_ref, out_ref, dq_ref):
    heads, group_rows, head = q_unit_ref.shape
    rows = group_rows // GROUP
    odd = lax.rem(lax.axis_index("ctx"), 2) == 1
    q_gain = gain_ref[...]

    def first(h):
        cols = columns(h, head)
        values = jnp.concatenate([v2_ref[:, cols], jnp.where(odd, v1a_ref[:, cols], v1b_ref[:, cols]), v0_ref[:, cols]], axis=0)
        d_normed = dqy_ref[h] * q_gain
        return dot(probs_ref[h].astype(BF16), values, ((0,), (0,))), d_normed, row_mean(d_normed * q_unit_ref[h])

    def second(h, result, d_normed, mean):
        d_q = (q_inv_ref[h] * (d_normed - q_unit_ref[h] * mean)).astype(BF16)
        result = result.astype(BF16)
        for j in range(GROUP):
            wide = columns(GROUP * h + j, head)
            out_ref[:, wide] = result[j * rows : (j + 1) * rows]
            dq_ref[:, wide] = d_q[j * rows : (j + 1) * rows]

    each_head(heads, first, second)


def merge_kernel(far_ref, *refs):
    near_refs, out_ref = refs[:-1], refs[-1]
    odd = lax.rem(lax.axis_index("ctx"), 2) == 1
    low = 0
    for near_ref in near_refs:
        cols = slice(low, low + near_ref.shape[1])
        near = jnp.where(odd, near_ref[...].astype(F32), 0.0)
        out_ref[:, cols] = (far_ref[:, cols].astype(F32) + near).astype(BF16)
        low = cols.stop


def finish_kernel(dy_ref, dv_ref, k1a_ref, k1b_ref, v1_ref, k2_ref, v2_ref, unit_ref, inv_ref, angle_ref, gain_ref, dk_out, dv_out):
    heads, rows, head = unit_ref.shape
    far = angle_ref.shape[1] - rows
    odd = lax.rem(lax.axis_index("ctx"), 2) == 1
    swap = swap_matrix(head)
    swaps = jnp.concatenate([swap, swap], axis=0)
    cosine, sine = angle_ref[0, far:], angle_ref[1, far:]
    gain = gain_ref[...]

    def first(h):
        cols = columns(h, head)
        near = jnp.where(odd, 0.0, v1_ref[:, cols].astype(F32))
        dv_out[:, cols] = (dv_ref[:, cols] + near + v2_ref[:, cols].astype(F32)).astype(BF16)
        k1_ref, low = (k1a_ref, h) if h < heads // 2 else (k1b_ref, h - heads // 2)
        near = jnp.where(odd, 0.0, k1_ref[:, columns(low, head)].astype(F32))
        rest = k2_ref[:, cols]
        return near + rest.astype(F32), dot(jnp.concatenate([near.astype(BF16), rest], axis=1), swaps)

    def second(h, both, swapped):
        d_y = dy_ref[:, columns(h, head)] + (both * cosine - swapped * sine)
        d_normed = d_y * gain
        return d_normed, row_mean(d_normed * unit_ref[h])

    def third(h, d_normed, mean):
        dk_out[:, columns(h, head)] = (inv_ref[h] * (d_normed - unit_ref[h] * mean)).astype(BF16)

    each_head(heads, first, second, third)


def share_kernel(own_ref, other_ref, out_ref):
    total = own_ref[...] + other_ref[...]
    head, size = total.shape[1], out_ref.shape[1]
    share = jnp.zeros(out_ref.shape, F32)
    for j in range(total.size // size):
        row, col = divmod(j * size, head)
        share = jnp.where(lax.axis_index("dp") == j, total[row : row + 1, col : col + size], share)
    out_ref[...] = share


def all_sum_term(value, axis, step):
    return lax.ppermute(value, axis, [(i, i ^ step) for i in range(lax.axis_size(axis))])


def all_sum(value, axis, steps):
    for step in steps:
        value = value + all_sum_term(value, axis, step)
    return value


def doublings(axis, first=1):
    count = lax.axis_size(axis)
    return [first << i for i in range(count.bit_length()) if first << i < count]


def on_device(q_proj, k_proj, v_proj, d_out, q_gain, k_gain):
    rows = q_proj.shape[1]
    head = q_gain.shape[0]
    heads = k_proj.shape[2] // head
    width = heads * head
    wide = GROUP * width
    span = WINDOW + rows
    far = WINDOW
    assert far == 2 * rows
    tall = GROUP * rows
    k2 = hop(k_proj, 2)
    v2 = ring_hop(v_proj, 2)
    k1_odd = swap_pairs(k_proj)
    v1_odd = swap_pairs(v_proj)

    half = head // 2
    freqs = jnp.power(ROPE_BASE, -2.0 * jnp.arange(half, dtype=F32) / head)
    sign = jnp.where(jnp.arange(head) < half, -1.0, 1.0)
    freqs = jnp.stack([jnp.tile(freqs, 2), sign])

    q_gain = q_gain.reshape(1, head)
    k_gain = k_gain.reshape(1, head)
    (angle_table,) = call(tables_kernel, "tables", [((2, span, head), F32)], (freqs,), flops=TABLES_COST)
    q_rot, q_unit, q_inv, k_rot, k_unit, k_inv, turn_table = call(
        prepare_kernel,
        "prepare",
        [((heads, tall, 2 * head), BF16), ((heads, tall, head), F32), ((heads, tall, head), F32)]
        + [((heads, rows, 2 * head), BF16), ((heads, rows, head), F32), ((heads, rows, head), F32)]
        + [((2, far, head), F32)],
        (q_proj[0], k_proj[0], q_gain, k_gain, angle_table),
    )
    q_rot, k2 = lax.optimization_barrier((q_rot, k2))
    k1 = k1_odd[0], swap_pairs(k2[0, :, : width // 2]), swap_pairs(k2[0, :, width // 2 :])
    probs, far_keys, far_unit, dv_own, dv1, dv2 = call(
        scores_kernel,
        "scores",
        [((heads, span, tall), F32), ((heads, far, 2 * head), BF16), ((heads, far, head), F32)]
        + [((rows, width), F32), ((rows, width), BF16), ((rows, width), BF16)],
        (q_rot, d_out[0], k_rot, *k1, k2[0], turn_table),
    )
    v2, dv1, dv2 = lax.optimization_barrier((v2, dv1, dv2))
    v1 = v1_odd[0], swap_pairs(v2)[0]
    dv_near = swap_pairs(dv1)
    (v_merged,) = call(merge_kernel, "merge_v", [((rows, width), BF16)], (dv2, dv_near))
    v_back = hop(v_merged, -2)
    dq_y, dy_own, dk1a, dk1b, dk2, gain_terms = call(
        grads_kernel,
        "grads",
        [((heads, tall, head), F32), ((rows, width), F32), ((rows, width // 2), BF16), ((rows, width // 2), BF16)]
        + [((rows, width), BF16), ((2, head), F32)],
        (probs, q_rot, q_unit, d_out[0], far_keys, k_rot, far_unit, k_unit, v_proj[0], *v1, v2[0], angle_table),
        scratch=[pltpu.VMEM((16, head), F32)],
    )
    dk_near = swap_pairs(dk1a), swap_pairs(dk1b)
    gain_terms = all_sum(gain_terms, "ctx", [1])
    gain_terms = all_sum(gain_terms, "ctx", [2])
    gain_terms, dk_near, v_back = lax.optimization_barrier((gain_terms, dk_near, v_back))
    (merged,) = call(merge_kernel, "merge_k", [((rows, width), BF16)], (dk2, *dk_near))
    k_back = hop(merged, -2)
    gain_terms = all_sum(gain_terms, "dp", doublings("dp"))
    result, d_q = call(
        outputs_kernel,
        "outputs",
        [((rows, wide), BF16), ((rows, wide), BF16)],
        (probs, v_proj[0], *v1, v2[0], dq_y, q_unit, q_inv, q_gain),
    )
    gain_terms, k_back, result, d_q = lax.optimization_barrier((gain_terms, k_back, result, d_q))
    *steps, last = doublings("ctx", 4)
    gain_terms = all_sum(gain_terms, "ctx", steps)
    others = all_sum_term(gain_terms, "ctx", last)
    d_k, d_v = call(
        finish_kernel,
        "finish",
        [((rows, width), BF16), ((rows, width), BF16)],
        (dy_own, dv_own, *dk_near, dv_near, k_back, v_back, k_unit, k_inv, angle_table, k_gain),
    )
    share = 2 * head // lax.axis_size("dp")
    (gain_share,) = call(share_kernel, "share", [((1, share), F32)], (gain_terms, others))
    return (result[None], d_q[None], d_k[None], d_v[None], gain_share[0])


def solution(mesh):
    tokens = P("dp", "ctx", None)
    return jax.shard_map(
        on_device,
        mesh=mesh,
        in_specs=(tokens,) * 4 + (P(), P()),
        out_specs=(tokens,) * 4 + (P("dp"),),
        check_vma=False,
    )
```
